32 devices in a mesh: dom: 8 (over z, y), grp: 4 (over x, core).
Axes of the slice: x: 2, y: 2, z: 4, core: 2. Of those that a mesh axis runs over, the one named last changes fastest.
Arguments:
- old_state: float32 [9, 56, 4096], P(None, None, ('dom', 'grp')), may hold values from -6 to 6
- stiffness: float32 [3, 56, 56], replicated, may hold values from -0.75 to 0.75
- jacobians: float32 [3, 9, 9, 4096], P(None, None, None, ('dom', 'grp')), may hold values from -2 to 2
- lift_own: float32 [4, 56, 56], replicated, may hold values from -0.75 to 0.75
- lift_across: float32 [4, 4, 56, 56], replicated, may hold values from -0.75 to 0.75
- riemann: float32 [2, 4, 9, 9, 4096], P(None, None, None, None, ('dom', 'grp')), may hold values from -2 to 2
- cluster_ids: int32 [4096], P(('dom', 'grp')), may hold values from 0 to 2
- send_slots: int32 [10240], P(('dom', 'grp')), may hold values from 0 to 127, as said below
- face_partner: int32 [4, 4096], P(None, ('dom', 'grp')), may hold values from 0 to 447, as said below
- partner_face: int32 [4, 4096], P(None, ('dom', 'grp')), may hold values from 0 to 3
- cohesion: float32 [4096], P(('dom', 'grp')), may hold values from 1 to 4
- relax_time: float32 [4096], P(('dom', 'grp')), may hold values from 0.1 to 1
- yield_flag: int32 [4096], P(('dom', 'grp')), may hold values 0 or 1
Outputs:
- new_state: float32 [9, 56, 4096], P(None, None, ('dom', 'grp'))
The draws below stay inside these ranges and needn't reach their ends.
Inputs may be any that keep to these rules, and one draw needn't show every extreme that they name: `send_slots`: local element numbers of the sending device; its first 256 slots go in equal shares to the devices of its grp group in grp order, the next 32 to the device one index lower along dom and the last 32 to the one one index higher, cyclically; the slots bound for one destination name distinct elements. `face_partner`: a place of the device's neighbour list: own elements, then what the grp group sends it, sender by sender, then what the lower and the higher dom neighbour send it; every received place is the partner of exactly one face of the device, all other faces have own places.
All inputs are finite; a program needn't handle non-finite values. No bound on the sum of `yield_flag` on one device may be relied on, other than what follows from the above.
Results may differ from the reference program's by a relative error of at most 0.0003.
Values sent between devices are 32-bit elements; how exact they have to be, the bound alone decides.
No kernel may reach another device: no remote copies, remote signals or barrier semaphores. Data moves between devices by JAX's collectives and lax.ppermute only.
A program may use at most 64 MiB of HBM per device.

```python
import math
import jax
import jax.numpy as jnp
from jax import lax

QUANT = 9
MODES = 56
ORDER = 6
ELEM_DEV = 128
GRP_SLOTS = 256
HALO = 32
ELEMS = 4096
SENDS = 10240
N_DOM = 8
N_GRP = 4


def distinct_orders(key, leading, count):
    scores = jax.random.randint(key, leading + (count,), 0, 1048576, dtype=jnp.int32)
    scores = scores * count + jnp.arange(count, dtype=jnp.int32)
    return jnp.argsort(scores, axis=-1).astype(jnp.int32)


def draw_send_slots(key, part):
    device_total = ELEMS // ELEM_DEV
    share = GRP_SLOTS // N_GRP
    peer_orders = distinct_orders(jax.random.fold_in(key, 11), (device_total, N_GRP), ELEM_DEV)
    peer_part = peer_orders[:, :, :share].reshape(device_total, GRP_SLOTS)
    lower_orders = distinct_orders(jax.random.fold_in(key, 12), (device_total,), ELEM_DEV)
    upper_orders = distinct_orders(jax.random.fold_in(key, 13), (device_total,), ELEM_DEV)
    whole = jnp.concatenate([peer_part, lower_orders[:, :HALO], upper_orders[:, :HALO]], axis=1)
    return whole.reshape(SENDS).astype(jnp.int32)


def draw_face_partner(key, part):
    device_total = ELEMS // ELEM_DEV
    faces = 4 * ELEM_DEV
    received = GRP_SLOTS + 2 * HALO
    order = distinct_orders(jax.random.fold_in(key, 21), (device_total,), faces)
    rank = jnp.argsort(order, axis=-1).astype(jnp.int32)
    local = jax.random.randint(jax.random.fold_in(key, 22), (device_total, faces), 0, ELEM_DEV, dtype=jnp.int32)
    places = jnp.where(rank < received, ELEM_DEV + rank, local)
    places = places.reshape(device_total, 4, ELEM_DEV)
    return jnp.transpose(places, (1, 0, 2)).reshape(4, ELEMS).astype(jnp.int32)


def with_ends(drawn, rng, least, largest):
    spot = [jax.random.randint(jax.random.fold_in(rng, axis), (), 0, length) for axis, length in enumerate(drawn.shape)]
    longest = drawn.shape.index(max(drawn.shape))
    beside = spot[:longest] + [(spot[longest] + 1) % drawn.shape[longest]] + spot[longest + 1:]
    return drawn.at[tuple(spot)].set(least).at[tuple(beside)].set(largest)


def steps_of(own_key, extent, cuts, smallest, high):
    factor_of = 1.0
    for position, parts in cuts:
        heights = jax.random.uniform(jax.random.fold_in(jax.random.fold_in(own_key, 6), position), (parts,), jnp.float32, smallest / len(cuts), high / len(cuts))
        factor_of = factor_of * jnp.repeat(jnp.exp(heights), extent[position] // parts).reshape((-1,) + (1,) * (len(extent) - 1 - position))
    return factor_of


def gaussian(key, shape, scale, most, split=(), kind=jnp.bfloat16):
    result = scale * jax.random.normal(key, shape, jnp.float32)
    if split:
        result = result * steps_of(key, shape, split, -0.22, 0.18)
    return jnp.clip(result, -most, most).astype(kind)


def setup_inputs(seed: int = 0) -> dict:
    key_of = jax.random.split(jax.random.key(seed), 14)
    return {
        "old_state": gaussian(key_of[0], (QUANT, MODES, ELEMS), 1.0, 6.0, ((2, 32),), jnp.float32),
        "stiffness": gaussian(key_of[1], (3, MODES, MODES), MODES ** -0.5, 0.75, (), jnp.float32),
        "jacobians": gaussian(key_of[2], (3, QUANT, QUANT, ELEMS), QUANT ** -0.5, 2.0, ((3, 32),), jnp.float32),
        "lift_own": gaussian(key_of[3], (4, MODES, MODES), MODES ** -0.5, 0.75, (), jnp.float32),
        "lift_across": gaussian(key_of[4], (4, 4, MODES, MODES), MODES ** -0.5, 0.75, (), jnp.float32),
        "riemann": gaussian(key_of[5], (2, 4, QUANT, QUANT, ELEMS), QUANT ** -0.5, 2.0, ((4, 32),), jnp.float32),
        "cluster_ids": with_ends(jax.random.randint(key_of[6], (ELEMS,), 0, 3), jax.random.fold_in(key_of[6], 1), 0, 2).astype(jnp.int32),
        "send_slots": draw_send_slots(jax.random.fold_in(key_of[13], 71), 0),
        "face_partner": draw_face_partner(jax.random.fold_in(key_of[13], 71), 0),
        "partner_face": with_ends(jax.random.randint(key_of[9], (4, ELEMS), 0, 4), jax.random.fold_in(key_of[9], 1), 0, 3).astype(jnp.int32),
        "cohesion": jnp.clip(1.0 + 3.0 * jax.random.uniform(key_of[10], (ELEMS,), jnp.float32) ** steps_of(key_of[10], (ELEMS,), ((0, 32),), -0.2, 0.2), 1.0, 4.0),
        "relax_time": jnp.clip(jnp.exp(math.log(1.0) - 2.3025851 * jax.random.uniform(key_of[11], (ELEMS,), jnp.float32) ** steps_of(key_of[11], (ELEMS,), ((0, 32),), -0.2, 0.2)), 0.1, 1.0),
        "yield_flag": with_ends((jax.random.randint(key_of[12], (ELEMS,), 0, 2) < 1).astype(jnp.int32), jax.random.fold_in(key_of[12], 1), 0, 1),
    }


base_step = 0.2
highest = lax.Precision.HIGHEST

def step_table(terms_count):
    entries = []
    for rate_level in range(3):
        interval = base_step * 2.0 ** rate_level
        factorial = 1.0
        powers = []
        for degree in range(terms_count):
            factorial = factorial * (degree + 1)
            powers.append(interval ** (degree + 1) / factorial)
        entries.append(powers)
    return jnp.array(entries, dtype=jnp.float32)

def clock_steps():
    return jnp.array([base_step, 2.0 * base_step, 4.0 * base_step], dtype=jnp.float32)

def cluster_selector(cluster_ids):
    return (cluster_ids[None, :] == jnp.arange(3, dtype=jnp.int32)[:, None]).astype(jnp.float32)

def on_modes(matrix, operand):
    return jnp.einsum('mn,qne->qme', matrix, operand, precision=highest)

def on_quantities(operand, blocks):
    return lax.optimization_barrier(jnp.sum(operand[:, None, :, :] * blocks[:, :, None, :], axis=0))

def taylor_stack(initial, stiffness, jacobian):
    collected = [initial]
    for degree in range(1, ORDER):
        latest = collected[-1]
        change = on_quantities(on_modes(stiffness[0], latest), jacobian[0])
        change = change + on_quantities(on_modes(stiffness[1], latest), jacobian[1])
        change = change + on_quantities(on_modes(stiffness[2], latest), jacobian[2])
        collected.append(-change)
    return jnp.stack(collected)

def integrate(stacked, weights):
    summed = weights[0] * stacked[0]
    for degree in range(1, stacked.shape[0]):
        summed = summed + weights[degree] * stacked[degree]
    return summed

def volume_term(own_int, stiffness, jacobian):
    summed = on_modes(stiffness[0].T, on_quantities(own_int, jacobian[0]))
    summed = summed + on_modes(stiffness[1].T, on_quantities(own_int, jacobian[1]))
    summed = summed + on_modes(stiffness[2].T, on_quantities(own_int, jacobian[2]))
    return summed

def face_update(own_int, neighbours, partner_sides, lift_own, lift_across, riemann):
    summed = jnp.zeros_like(own_int)
    candidates = jnp.arange(4, dtype=jnp.int32)[:, None]
    for face_index in range(4):
        summed = summed + on_quantities(on_modes(lift_own[face_index], own_int), riemann[0, face_index])
        projected = jnp.einsum('jmn,qne->qjme', lift_across[face_index], neighbours[face_index], precision=highest)
        picker = (partner_sides[face_index][None, :] == candidates).astype(jnp.float32)
        chosen = lax.optimization_barrier(jnp.sum(projected * picker[None, :, None, :], axis=1))
        summed = summed + on_quantities(chosen, riemann[1, face_index])
    return summed

def plastic(updated, cohesion, relax_time, yielding, interval):
    isotropic = (jnp.arange(6, dtype=jnp.int32) < 3).astype(jnp.float32)[:, None, None]
    pressure = (updated[0] + updated[1] + updated[2]) / 3.0
    deviator = updated[:6] - isotropic * pressure[None]
    centre = deviator[:, 0, :]
    second = 0.5 * (centre[0] * centre[0] + centre[1] * centre[1] + centre[2] * centre[2])
    second = second + centre[3] * centre[3] + centre[4] * centre[4] + centre[5] * centre[5]
    strength = jnp.sqrt(second)
    excess = jnp.maximum(strength - cohesion, 0.0) / jnp.maximum(strength, cohesion)
    factor = yielding.astype(jnp.float32) * excess * (1.0 - jnp.exp(-interval / relax_time))
    return jnp.concatenate([updated[:6] - factor[None, None, :] * deviator, updated[6:]], axis=0)

def advance(own_block, stiffness, jacobian, lift_own, lift_across, riemann, selector, own_int, neighbours, partner_sides, cohesion, relax_time, yielding):
    updated = own_block + volume_term(own_int, stiffness, jacobian)
    updated = updated - face_update(own_int, neighbours, partner_sides, lift_own, lift_across, riemann)
    interval = lax.optimization_barrier(jnp.sum(selector * clock_steps()[:, None], axis=0))
    return plastic(updated, cohesion, relax_time, yielding, interval)

def reference(old_state, stiffness, jacobians, lift_own, lift_across, riemann, cluster_ids, send_slots, face_partner, partner_face, cohesion, relax_time, yield_flag):
    device_total = N_DOM * N_GRP
    per_device = ELEM_DEV
    peer_slots = GRP_SLOTS // N_GRP
    sent_count = GRP_SLOTS + 2 * HALO
    taylor_table = step_table(ORDER)
    sends = send_slots.reshape(device_total, sent_count)

    def predict(device):
        offset = (device * per_device).astype(jnp.int32)
        own_block = lax.dynamic_slice_in_dim(old_state, offset, per_device, 2)
        jacobian = lax.dynamic_slice_in_dim(jacobians, offset, per_device, 3)
        collected = taylor_stack(own_block, stiffness, jacobian)
        return jnp.stack([integrate(collected, taylor_table[rate_level][:, None]) for rate_level in range(3)])
    device_ids = jnp.arange(device_total, dtype=jnp.int32)
    levels = lax.map(predict, device_ids)

    def update(device):
        offset = (device * per_device).astype(jnp.int32)
        dom_index = device // N_GRP
        grp_index = device % N_GRP
        peer_ids = dom_index * N_GRP + jnp.arange(N_GRP, dtype=jnp.int32)
        peer_devices = jnp.repeat(peer_ids, peer_slots)
        peer_columns = grp_index * peer_slots + jnp.tile(jnp.arange(peer_slots, dtype=jnp.int32), N_GRP)
        peer_elements = sends[peer_devices, peer_columns]
        below = (dom_index + N_DOM - 1) % N_DOM * N_GRP + grp_index
        above = (dom_index + 1) % N_DOM * N_GRP + grp_index
        rim_range = jnp.arange(HALO, dtype=jnp.int32)
        below_elements = sends[below, GRP_SLOTS + HALO + rim_range]
        above_elements = sends[above, GRP_SLOTS + rim_range]
        source_device = jnp.concatenate([jnp.full((per_device,), device, jnp.int32), peer_devices, jnp.full((HALO,), below, jnp.int32), jnp.full((HALO,), above, jnp.int32)])
        source_element = jnp.concatenate([jnp.arange(per_device, dtype=jnp.int32), peer_elements, below_elements, above_elements])
        own_clusters = lax.dynamic_slice_in_dim(cluster_ids, offset, per_device, 0)
        selector = cluster_selector(own_clusters)
        own_int = lax.optimization_barrier(jnp.sum(levels[device] * selector[:, None, None, :], axis=0))
        partners = lax.dynamic_slice_in_dim(face_partner, offset, per_device, 1)
        partner_sides = lax.dynamic_slice_in_dim(partner_face, offset, per_device, 1)
        neighbours = []
        for face_index in range(4):
            owner_ids = source_device[partners[face_index]]
            element_ids = source_element[partners[face_index]]
            picked = jnp.transpose(levels[owner_ids, :, :, :, element_ids], (1, 2, 3, 0))
            neighbours.append(lax.optimization_barrier(jnp.sum(picked * selector[:, None, None, :], axis=0)))
        own_block = lax.dynamic_slice_in_dim(old_state, offset, per_device, 2)
        jacobian = lax.dynamic_slice_in_dim(jacobians, offset, per_device, 3)
        solvers = lax.dynamic_slice_in_dim(riemann, offset, per_device, 4)
        return advance(own_block, stiffness, jacobian, lift_own, lift_across, solvers, selector, own_int, neighbours, partner_sides, lax.dynamic_slice_in_dim(cohesion, offset, per_device, 0), lax.dynamic_slice_in_dim(relax_time, offset, per_device, 0), lax.dynamic_slice_in_dim(yield_flag, offset, per_device, 0))
    results = lax.map(update, device_ids)
    return jnp.transpose(results, (1, 2, 0, 3)).reshape(QUANT, MODES, ELEMS)
```

```python
import jax
import jax.numpy as jnp
from jax import lax
from jax.experimental import pallas as pl
from jax.experimental.pallas import tpu as pltpu
from jax.sharding import PartitionSpec as P

QUANT = 9
MODES = 56
ORDER = 6
GRP_SLOTS = 256
HALO = 32
LEVELS = 3
LANES = 128
SUB = 8
ROWS = QUANT * MODES

base_step = 0.2
f32 = jnp.float32
bf16 = jnp.bfloat16
VMEM_LIMIT = 24 << 20


def round_up(value, unit):
    return -(-value // unit) * unit


def rows_per_group(total, width):
    return round_up(-(-total // (LANES // width)), SUB)


LEVEL_ROWS = round_up(LEVELS * ROWS, 4 * SUB)


def pack3_rows():
    return rows_per_group(LEVELS * ROWS, HALO)


def take(block, idx):
    return jnp.take_along_axis(
        block, jnp.broadcast_to(idx, block.shape), axis=1, mode="promise_in_bounds"
    )


def pick(ref, position):
    lane = jnp.bitwise_and(position, LANES - 1)
    tile = jnp.right_shift(position, 7)
    out = take(ref[:, 0:LANES], lane)
    for v in range(1, ref.shape[1] // LANES):
        out = jnp.where(tile == v, take(ref[:, v * LANES : (v + 1) * LANES], lane), out)
    return out


def lane_ids():
    return lax.broadcasted_iota(jnp.int32, (SUB, LANES), 1)


def device_place():
    grp = lax.axis_index("grp")
    odd = jnp.bitwise_and(lax.axis_index("dom"), 1)
    return grp, odd


def bases(n_grp):
    grp, odd = device_place()
    width = GRP_SLOTS // n_grp
    found = [(jnp.bitwise_xor(grp, k) * width, width) for k in range(1, n_grp)]
    found.append((GRP_SLOTS + HALO * (1 - odd), HALO))
    found.append((GRP_SLOTS + HALO * odd, HALO))
    return found


def split(x):
    high = x.astype(bf16).astype(f32)
    return high, x - high


def stationary(x):
    high, low = split(x)
    return jnp.concatenate([high, low, high], axis=0).astype(bf16)


def streamed(w):
    high, low = split(w)
    return jnp.concatenate([high, high, low], axis=1).astype(bf16)


def matmul(w, x):
    return jnp.dot(w, x, preferred_element_type=f32)


def row8(ref, index, sub):
    return jnp.broadcast_to(ref[(*index, pl.ds(sub, 1), slice(None))], (SUB, LANES))


def tiles(x):
    return x.reshape(x.shape[0] // SUB, SUB, LANES)


def untile(x):
    return x.reshape(x.shape[0] * SUB, LANES)


def request_kernel(n_grp, partner_ref, cluster_ref, *rest):
    outs, row_ref = rest[:-1], rest[-1]
    received = GRP_SLOTS + 2 * HALO
    owned = cluster_ref.shape[1]
    place = lax.broadcasted_iota(jnp.int32, (received, LANES), 0) + owned
    cluster = cluster_ref[...].astype(f32)
    marks = jnp.zeros((received, LANES), f32)
    for f in range(4):
        marks = jnp.where(partner_ref[f : f + 1, :] == place, cluster, marks)
    rows = lax.dot_general(
        jnp.ones((SUB, LANES), bf16),
        marks.astype(bf16),
        (((1,), (1,)), ((), ())),
        preferred_element_type=f32,
    )
    row_ref[...] = jnp.zeros(row_ref.shape, jnp.int32)
    row_ref[:, :received] = rows.astype(jnp.int32)
    lane = lane_ids()
    for out, (base, width) in zip(outs, bases(n_grp)):
        out[...] = pick(row_ref, base + jnp.bitwise_and(lane, width - 1))


def predictor_kernel(state_ref, stiff_ref, jac_ref, level_ref, w_ref, rhs_ref, y0_ref, y1_ref):
    w_ref[...] = streamed(stiff_ref[...].reshape(3 * MODES, MODES))
    level_ref[pl.ds(LEVELS * ROWS, LEVEL_ROWS - LEVELS * ROWS), :] = jnp.zeros(
        (LEVEL_ROWS - LEVELS * ROWS, LANES), f32
    )

    def column(q):
        return pl.ds(q * LANES, LANES)

    def project(y_ref, first, last):
        span = pl.ds(first * LANES, (last - first) * LANES)
        y_ref[:, span] = matmul(w_ref[...], rhs_ref[:, span])

    for q in range(QUANT):
        v = state_ref[q] * base_step
        rhs_ref[:, column(q)] = stationary(v)
        for c in range(LEVELS):
            level_ref[pl.ds(c * ROWS + q * MODES, MODES), :] = v * 2.0**c
        if q % 2 == 1 or q == QUANT - 1:
            project(y0_ref, q - q % 2, q + 1)
    for degree in range(1, ORDER):
        y_ref, next_ref = (y0_ref, y1_ref) if degree % 2 == 1 else (y1_ref, y0_ref)
        factor = -base_step / (degree + 1)
        for q in range(QUANT):
            acc = None
            for p in range(QUANT):
                for d in range(3):
                    term = tiles(y_ref[d * MODES : (d + 1) * MODES, column(p)]) * row8(jac_ref, (p, q), d)
                    acc = term if acc is None else acc + term
            v = untile(acc) * factor
            for c in range(LEVELS):
                rows = pl.ds(c * ROWS + q * MODES, MODES)
                level_ref[rows, :] = level_ref[rows, :] + v * 2.0 ** (c * (degree + 1))
            if degree < ORDER - 1:
                rhs_ref[:, column(q)] = stationary(v)
                if q % 2 == 1 or q == QUANT - 1:
                    project(next_ref, q - q % 2, q + 1)


def send_kernel(n_grp, level_ref, slot_ref, *rest):
    n_req = n_grp
    reqs, outs, row_ref = rest[:n_req], rest[n_req:-1], rest[-1]
    row_ref[...] = jnp.zeros(row_ref.shape, jnp.int32)
    row_ref[:, : slot_ref.shape[1]] = jnp.broadcast_to(slot_ref[...], (SUB, slot_ref.shape[1]))
    lane = lane_ids()
    for k, (base, width) in enumerate(bases(n_grp)):
        idx = pick(row_ref, base + jnp.bitwise_and(lane, width - 1))[:1]
        group = jnp.right_shift(lane, width.bit_length() - 1)[:1]
        height = outs[k].shape[0]
        out = None
        for g in range(LANES // width):
            if k < n_req:
                want = reqs[k][0:1, :]
                rows = min(height, ROWS - g * height)
                part = take(level_ref[pl.ds(g * height, rows), :], idx)
                for c in range(1, LEVELS):
                    other = take(level_ref[pl.ds(c * ROWS + g * height, rows), :], idx)
                    part = jnp.where(want == c, other, part)
            else:
                rows = min(height, LEVEL_ROWS - g * height)
                part = take(level_ref[pl.ds(g * height, rows), :], idx)
            if rows < height:
                part = jnp.concatenate([part, jnp.zeros((height - rows, LANES), f32)], axis=0)
            out = part if out is None else jnp.where(group == g, part, out)
        outs[k][...] = out


def own_kernel(
    n_grp, level_ref, state_ref, stiff_ref, jac_ref, lift_ref, across_ref, riem_ref,
    cluster_ref, slot_ref, partner_ref, part_ref, near_ref, wa_ref,
    row_ref, w_ref, rhs_ref, y_ref,
):
    cluster = cluster_ref[...]
    for q in range(QUANT):
        own = level_ref[pl.ds(q * MODES, MODES), :]
        for c in range(1, LEVELS):
            own = jnp.where(cluster == c, level_ref[pl.ds(c * ROWS + q * MODES, MODES), :], own)
        rhs_ref[:, pl.ds(q * LANES, LANES)] = stationary(own)
    for d in range(3):
        w_ref[pl.ds(d * MODES, MODES), :] = streamed(stiff_ref[d].T)
    w_ref[pl.ds(3 * MODES, 4 * MODES), :] = streamed(lift_ref[...].reshape(4 * MODES, MODES))
    for q in range(0, QUANT, 2):
        span = pl.ds(q * LANES, min(2, QUANT - q) * LANES)
        y_ref[:, span] = matmul(w_ref[...], rhs_ref[:, span])
    for q in range(QUANT):
        acc = tiles(state_ref[q])
        for p in range(QUANT):
            for d in range(3):
                term = tiles(y_ref[pl.ds(d * MODES, MODES), pl.ds(p * LANES, LANES)])
                acc = acc + term * row8(jac_ref, (p, q), d)
            for f in range(4):
                term = tiles(y_ref[pl.ds((3 + f) * MODES, MODES), pl.ds(p * LANES, LANES)])
                acc = acc - term * row8(riem_ref, (0, p, q), f)
        part_ref[q] = untile(acc)
    row_ref[...] = jnp.zeros(row_ref.shape, jnp.int32)
    row_ref[:, : slot_ref.shape[1]] = jnp.broadcast_to(slot_ref[...], (SUB, slot_ref.shape[1]))
    owned = cluster_ref.shape[1]
    for f in range(4):
        place = jnp.broadcast_to(partner_ref[f : f + 1, :], (SUB, LANES))
        inside = place < owned
        slot = jnp.maximum(place - owned, 0)
        idx = jnp.where(inside, place, pick(row_ref, slot))[:1]
        for q in range(QUANT):
            near = take(level_ref[pl.ds(q * MODES, MODES), :], idx)
            for c in range(1, LEVELS):
                other = take(level_ref[pl.ds(c * ROWS + q * MODES, MODES), :], idx)
                near = jnp.where(cluster == c, other, near)
            near_ref[f, pl.ds(q * MODES, MODES), :] = near
        wa_ref[f] = streamed(across_ref[f].reshape(4 * MODES, MODES))


def final_kernel(n_grp, *refs):
    n_got = n_grp + 1
    gots = refs[:n_got]
    (part_ref, near_ref, wa_ref, riem_ref, cluster_ref, partner_ref, side_ref,
     cohesion_ref, relax_ref, yield_ref, out_ref, rhs_ref, z_ref, chosen_ref) = refs[n_got:]
    owned = cluster_ref.shape[1]
    cluster = cluster_ref[...]
    table = bases(n_grp)

    def unpack(got_ref, width, first, rows, idx):
        height = got_ref.shape[0]
        parts = []
        at = first
        while at < first + rows:
            g, off = at // height, at % height
            n = min(height - off, first + rows - at)
            parts.append(take(got_ref[pl.ds(off, n), :], idx + g * width))
            at += n
        return parts[0] if len(parts) == 1 else jnp.concatenate(parts, axis=0)

    for f in range(4):
        slot = partner_ref[f : f + 1, :] - owned
        plans = []
        for k, (base, width) in enumerate(table):
            rel = slot - base
            hit = jnp.logical_and(rel >= 0, rel < width)
            plans.append((gots[k], width, hit, jnp.bitwise_and(rel, width - 1)))
        for q in range(QUANT):
            near = near_ref[f, pl.ds(q * MODES, MODES), :]
            for k, (got, width, hit, idx) in enumerate(plans):
                if k < n_grp:
                    near = jnp.where(hit, unpack(got, width, q * MODES, MODES, idx), near)
                else:
                    for c in range(LEVELS):
                        mine = jnp.logical_and(hit, cluster == c)
                        near = jnp.where(
                            mine, unpack(got, width, c * ROWS + q * MODES, MODES, idx), near
                        )
            rhs_ref[:, pl.ds(q * LANES, LANES)] = stationary(near)
        side = side_ref[f : f + 1, :]
        for q in range(0, QUANT, 2):
            n = min(2, QUANT - q)
            span = pl.ds(q * LANES, n * LANES)
            z_ref[:, span] = matmul(wa_ref[f], rhs_ref[:, span])
            for p in range(q, q + n):
                cut = pl.ds(p * LANES, LANES)
                chosen = z_ref[pl.ds(0, MODES), cut]
                for j in range(1, 4):
                    chosen = jnp.where(side == j, z_ref[pl.ds(j * MODES, MODES), cut], chosen)
                chosen_ref[f, p] = chosen
    updated = []
    for q in range(QUANT):
        acc = tiles(part_ref[q])
        for f in range(4):
            for p in range(QUANT):
                acc = acc - tiles(chosen_ref[f, p]) * row8(riem_ref, (1, p, q), f)
        out_ref[q] = untile(acc)
    heads = [out_ref[q, 0:1, :] for q in range(6)]
    mean = (heads[0] + heads[1] + heads[2]) / 3.0
    dev = [heads[q] - mean if q < 3 else heads[q] for q in range(6)]
    second = 0.5 * (dev[0] * dev[0] + dev[1] * dev[1] + dev[2] * dev[2])
    second = second + dev[3] * dev[3] + dev[4] * dev[4] + dev[5] * dev[5]
    strength = jnp.sqrt(second)
    cohesion = cohesion_ref[...]
    step = jnp.where(cluster == 0, base_step, jnp.where(cluster == 1, 2.0 * base_step, 4.0 * base_step))
    excess = jnp.maximum(strength - cohesion, 0.0) / jnp.maximum(strength, cohesion)
    factor = yield_ref[...].astype(f32) * excess * (1.0 - jnp.exp(-step / relax_ref[...]))
    pressure = (out_ref[0] + out_ref[1] + out_ref[2]) / 3.0
    for q in range(6):
        now = out_ref[q]
        out_ref[q] = now - factor * (now - pressure if q < 3 else now)


def call(kernel, out_shape, scratch, *args, cost=None, name=None):
    vmem = pl.BlockSpec(memory_space=pltpu.VMEM)
    many = isinstance(out_shape, (list, tuple))
    return pl.pallas_call(
        kernel,
        out_shape=out_shape,
        in_specs=[vmem] * len(args),
        out_specs=[vmem] * len(out_shape) if many else vmem,
        scratch_shapes=scratch,
        compiler_params=pltpu.CompilerParams(vmem_limit_bytes=VMEM_LIMIT),
        cost_estimate=cost,
        name=name,
    )(*args)


def on_device(
    n_dom, n_grp, old_state, stiffness, jacobians, lift_own, lift_across, riemann,
    cluster_ids, send_slots, face_partner, partner_face, cohesion, relax_time, yield_flag,
):
    owned = old_state.shape[2]
    slots = send_slots.shape[0]
    wide = round_up(slots, LANES)
    shape = jax.ShapeDtypeStruct
    width = GRP_SLOTS // n_grp
    jac = jnp.transpose(jacobians, (1, 2, 0, 3))
    riem = jnp.transpose(riemann, (0, 2, 3, 1, 4))
    cluster = cluster_ids.reshape(1, owned)
    slot_row = send_slots.reshape(1, slots)

    pair_low = [(i, i ^ 1) for i in range(n_dom)]
    pair_high = [(i, ((i + 1) if i % 2 else (i - 1)) % n_dom) for i in range(n_dom)]
    routes = [("grp", [(i, i ^ k) for i in range(n_grp)]) for k in range(1, n_grp)]
    routes += [("dom", pair_low), ("dom", pair_high)]
    order = sorted(range(n_grp - 1), key=lambda k: (k + 1) < 2) + [n_grp - 1]

    def request_body(*refs):
        request_kernel(n_grp, *refs)

    requests = call(
        request_body,
        [shape((SUB, LANES), jnp.int32)] * n_grp,
        [pltpu.VMEM((SUB, wide), jnp.int32)],
        face_partner, cluster, name="requests",
    )
    wanted = [None] * n_grp
    for k in order:
        wanted[k] = lax.ppermute(requests[k], *routes[k])

    levels = call(
        predictor_kernel,
        shape((LEVEL_ROWS, LANES), f32),
        [
            pltpu.VMEM((3 * MODES, 3 * MODES), bf16),
            pltpu.VMEM((3 * MODES, QUANT * LANES), bf16),
            pltpu.VMEM((3 * MODES, QUANT * LANES), f32),
            pltpu.VMEM((3 * MODES, QUANT * LANES), f32),
        ],
        old_state, stiffness, jac, name="predictor",
    )

    heights = [rows_per_group(ROWS, width)] * (n_grp - 1)
    heights += [rows_per_group(ROWS, HALO), pack3_rows()]

    def send_body(*refs):
        send_kernel(n_grp, *refs)

    outgoing = call(
        send_body,
        [shape((h, LANES), f32) for h in heights],
        [pltpu.VMEM((SUB, wide), jnp.int32)],
        levels, slot_row, *wanted, name="sends",
    )
    gots = [None] * (n_grp + 1)
    for k in order + [n_grp]:
        gots[k] = lax.ppermute(outgoing[k], *routes[k])

    def own_body(*refs):
        own_kernel(n_grp, *refs)

    partial, near, across = call(
        own_body,
        [
            shape((QUANT, MODES, LANES), f32),
            shape((4, ROWS, LANES), f32),
            shape((4, 4 * MODES, 3 * MODES), bf16),
        ],
        [
            pltpu.VMEM((SUB, wide), jnp.int32),
            pltpu.VMEM((7 * MODES, 3 * MODES), bf16),
            pltpu.VMEM((3 * MODES, QUANT * LANES), bf16),
            pltpu.VMEM((7 * MODES, QUANT * LANES), f32),
        ],
        levels, old_state, stiffness, jac, lift_own, lift_across, riem, cluster, slot_row,
        face_partner,
        cost=pl.CostEstimate(flops=10**8, bytes_accessed=4 * 10**6, transcendentals=0),
        name="own",
    )

    def final_body(*refs):
        final_kernel(n_grp, *refs)

    return call(
        final_body,
        shape((QUANT, MODES, LANES), f32),
        [
            pltpu.VMEM((3 * MODES, QUANT * LANES), bf16),
            pltpu.VMEM((4 * MODES, QUANT * LANES), f32),
            pltpu.VMEM((4, QUANT, MODES, LANES), f32),
        ],
        *gots, partial, near, across, riem, cluster, face_partner, partner_face,
        cohesion.reshape(1, owned), relax_time.reshape(1, owned), yield_flag.reshape(1, owned),
        name="final",
    )


def solution(mesh):
    n_dom, n_grp = mesh.shape["dom"], mesh.shape["grp"]
    both = ("dom", "grp")
    in_specs = (
        P(None, None, both), P(), P(None, None, None, both), P(), P(),
        P(None, None, None, None, both), P(both), P(both), P(None, both), P(None, both),
        P(both), P(both), P(both),
    )

    def body(*args):
        return on_device(n_dom, n_grp, *args)

    return jax.shard_map(
        body, mesh=mesh, in_specs=in_specs, out_specs=P(None, None, both), check_vma=False
    )
```

```python
import jax
import jax.numpy as jnp
from jax import lax
from jax.experimental import pallas as pl
from jax.experimental.pallas import tpu as pltpu
from jax.sharding import PartitionSpec as P

QUANT = 9
MODES = 56
ORDER = 6
GRP_SLOTS = 256
HALO = 32
LEVELS = 3
LANES = 128
SUB = 8
MT = MODES // SUB
VT = QUANT * MT
VP = 64
GROUP = 3

base_step = 0.2
f32 = jnp.float32
bf16 = jnp.bfloat16
i32 = jnp.int32
VMEM_LIMIT = 24 << 20


def round_up(value, unit):
    return -(-value // unit) * unit


class Plan:
    def __init__(self, n_dom, n_grp):
        share = GRP_SLOTS // n_grp
        self.n_grp = n_grp
        self.width = [HALO, HALO] + [share] * (n_grp - 1)
        pairs = [(i, i ^ 1) for i in range(n_dom)]
        others = [(i, ((i + 1) if i % 2 else (i - 1)) % n_dom) for i in range(n_dom)]
        self.route = [("dom", pairs), ("dom", others)]
        self.route += [("grp", [(i, i ^ k) for i in range(n_grp)]) for k in range(1, n_grp)]
        self.reg, self.start = [], []
        at = 0
        for w in self.width:
            at = round_up(at, w)
            self.reg.append(at // LANES)
            self.start.append(at % LANES)
            at += w
        self.n_reg = -(-at // LANES)
        self.count = len(self.width)
        self.full = [k == 1 for k in range(self.count)]
        narrow = min(self.width)
        self.shift = narrow.bit_length() - 1
        self.masks = LANES // narrow
        self.order = [k for k in range(3, self.count)] + [0, 2]

    def chunk(self, k):
        return VP * self.width[k] // LANES

    def height(self, k):
        return self.chunk(k) * (LEVELS if self.full[k] else 1)

    def mask_id(self, v):
        return v * self.masks // VP

    def members(self, reg):
        return [k for k in range(self.count) if self.reg[k] == reg]

    def bases(self):
        grp = lax.axis_index("grp")
        odd = jnp.bitwise_and(lax.axis_index("dom"), 1)
        found = [GRP_SLOTS + HALO * (1 - odd), GRP_SLOTS + HALO * odd]
        for k in range(1, self.n_grp):
            found.append(jnp.bitwise_xor(grp, k) * self.width[k + 1])
        return found


def take(x, idx):
    flat = x.reshape(-1, LANES)
    wide = jnp.broadcast_to(idx[None], (flat.shape[0] // SUB, SUB, LANES)).reshape(flat.shape)
    out = jnp.take_along_axis(flat, wide, axis=1, mode="promise_in_bounds")
    return out.reshape(x.shape)


def pick(ref, position):
    lane = jnp.bitwise_and(position, LANES - 1)
    tile = jnp.right_shift(position, 7)
    out = take(ref[:, 0:LANES], lane)
    for v in range(1, ref.shape[1] // LANES):
        out = jnp.where(tile == v, take(ref[:, v * LANES : (v + 1) * LANES], lane), out)
    return out


def lane_ids():
    return lax.broadcasted_iota(i32, (SUB, LANES), 1)


def spread(row):
    return jnp.broadcast_to(row, (SUB, row.shape[-1]))


def split(x):
    high = x.astype(bf16).astype(f32)
    return high, x - high


def stationary(x):
    high, low = split(x.reshape(MODES, x.shape[-1]))
    return jnp.concatenate([high, low, high], axis=0).astype(bf16)


def streamed(w):
    high, low = split(w)
    return jnp.concatenate([high, high, low], axis=1).astype(bf16)


def matmul(w, x):
    return jnp.dot(w, x, preferred_element_type=f32)


def row8(ref, index, sub):
    return spread(ref[(*index, pl.ds(sub, 1), slice(None))])


def quantity(q):
    return pl.ds(q * MT, MT)


def request_kernel(plan, *refs):
    n_load = 3
    partner_hbm, cluster_hbm = refs[0:2]
    bulk_hbm = refs[2 : 2 + n_load]
    rest = refs[2 + n_load :]
    outs, rest = rest[: plan.count], rest[plan.count :]
    bulk_out, rest = rest[:n_load], rest[n_load:]
    partner_ref, cluster_ref, row_ref, sems = rest
    copies = [
        pltpu.make_async_copy(partner_hbm, partner_ref, sems.at[0]),
        pltpu.make_async_copy(cluster_hbm, cluster_ref, sems.at[1]),
    ]
    copies += [
        pltpu.make_async_copy(a, b, sems.at[2 + i]) for i, (a, b) in enumerate(zip(bulk_hbm, bulk_out))
    ]
    for copy in copies:
        copy.start()
    for copy in copies[:2]:
        copy.wait()
    received = GRP_SLOTS + 2 * HALO
    owned = cluster_ref.shape[1]
    place = lax.broadcasted_iota(i32, (received, LANES), 0) + owned
    cluster = cluster_ref[...].astype(f32)
    marks = jnp.zeros((received, LANES), f32)
    for f in range(4):
        marks = jnp.where(partner_ref[f : f + 1, :] == place, cluster, marks)
    rows = lax.dot_general(
        jnp.ones((SUB, LANES), bf16),
        marks.astype(bf16),
        (((1,), (1,)), ((), ())),
        preferred_element_type=f32,
    )
    row_ref[...] = jnp.zeros(row_ref.shape, i32)
    row_ref[:, :received] = rows.astype(i32)
    lane = lane_ids()
    for out, base, width in zip(outs, plan.bases(), plan.width):
        out[...] = pick(row_ref, base + jnp.bitwise_and(lane, width - 1))
    for copy in copies[2:]:
        copy.wait()


def predictor_kernel(state_ref, stiff_ref, jac_ref, level_ref, w_ref, rhs_ref, y0_ref, y1_ref):
    w_ref[...] = streamed(stiff_ref[...].reshape(3 * MODES, MODES))
    level_ref[:, pl.ds(VT, VP - VT)] = jnp.zeros((LEVELS, VP - VT, SUB, LANES), f32)
    steps = QUANT // GROUP

    def project(y_ref, g):
        y = matmul(w_ref[...], rhs_ref[g])
        for i in range(GROUP):
            y_ref[g, i] = y[:, i * LANES : (i + 1) * LANES].reshape(3 * MT, SUB, LANES)

    for q in range(QUANT):
        v = state_ref[q].reshape(MT, SUB, LANES) * base_step
        rhs_ref[1 + q // GROUP, :, pl.ds(q % GROUP * LANES, LANES)] = stationary(v)
        for c in range(LEVELS):
            level_ref[c, quantity(q)] = v * 2.0**c
    for g in range(steps):
        project(y0_ref, g + 1)
    for degree in range(1, ORDER):
        y_ref, next_ref = (y0_ref, y1_ref) if degree % 2 == 1 else (y1_ref, y0_ref)
        factor = -base_step / (degree + 1)
        last = degree == ORDER - 1

        def body(g, carry, y_ref=y_ref, next_ref=next_ref, factor=factor, last=last, degree=degree):
            if not last:
                project(next_ref, g)
            acc = [None] * GROUP
            for p in range(QUANT):
                for d in range(3):
                    y = y_ref[1 + p // GROUP, p % GROUP, pl.ds(d * MT, MT)]
                    for i in range(GROUP):
                        term = y * row8(jac_ref, (p, g * GROUP + i), d)
                        acc[i] = term if acc[i] is None else acc[i] + term
            for i in range(GROUP):
                v = acc[i] * factor
                at = pl.ds((g * GROUP + i) * MT, MT)
                for c in range(LEVELS):
                    level_ref[c, at] = level_ref[c, at] + v * 2.0 ** (c * (degree + 1))
                if not last:
                    rhs_ref[g + 1, :, pl.ds(i * LANES, LANES)] = stationary(v)
            return carry

        lax.fori_loop(0, steps, body, 0)
        if not last:
            project(next_ref, steps)


def send_kernel(plan, reg, level_ref, slot_ref, *rest):
    mine = plan.members(reg)
    asked = [k for k in mine if not plan.full[k]]
    reqs = dict(zip(asked, rest[: len(asked)]))
    outs = dict(zip(mine, rest[len(asked) : -1]))
    row_ref = rest[-1]
    row_ref[...] = jnp.zeros(row_ref.shape, i32)
    row_ref[:, : slot_ref.shape[1]] = spread(slot_ref[...])
    lane = lane_ids()
    bases = plan.bases()
    index = jnp.zeros((SUB, LANES), i32)
    want = jnp.zeros((SUB, LANES), i32)
    for k in mine:
        w = plan.width[k]
        inside = jnp.right_shift(lane, w.bit_length() - 1) == plan.start[k] // w
        index = jnp.where(inside, pick(row_ref, bases[k] + jnp.bitwise_and(lane, w - 1)), index)
        if k in reqs:
            want = jnp.where(inside, reqs[k][...], want)
    swap = [jnp.bitwise_xor(lane, m << plan.shift) for m in range(plan.masks)]
    indices = [index] + [take(index, s) for s in swap[1:]]
    wants = [want] + [take(want, s) for s in swap[1:]]
    block = {k: jnp.right_shift(lane, plan.width[k].bit_length() - 1) for k in mine}
    widest = max(plan.chunk(k) for k in mine)
    narrowest = min(plan.chunk(k) for k in mine)
    for u in range(narrowest):
        plain, chosen = {}, {}
        for v in range(u, VP, narrowest):
            m = plan.mask_id(v)
            plain[v] = [take(level_ref[c, v], indices[m]) for c in range(LEVELS)]
            got = plain[v][0]
            for c in range(1, LEVELS):
                got = jnp.where(wants[m] == c, plain[v][c], got)
            chosen[v] = got
        for k in mine:
            chunk = plan.chunk(k)
            n_block = LANES // plan.width[k]
            first = plan.start[k] // plan.width[k]
            for w in range(u, chunk, narrowest):
                for c in range(LEVELS if plan.full[k] else 1):
                    out = None
                    for j in range(n_block):
                        v = (j ^ first) * chunk + w
                        part = plain[v][c] if plan.full[k] else chosen[v]
                        out = part if out is None else jnp.where(block[k] == j, part, out)
                    outs[k][c * chunk + w] = out


def own_kernel(
    plan, level_ref, state_ref, stiff_ref, jac_ref, lift_ref, across_ref, riem_ref,
    cluster_ref, slot_ref, partner_ref, relax_ref, yield_ref,
    part_ref, near_ref, wa_ref, gain_ref,
    row_ref, w_ref, rhs_ref, y_ref,
):
    cluster = spread(cluster_ref[...])
    for q in range(QUANT):
        own = level_ref[0, quantity(q)]
        for c in range(1, LEVELS):
            own = jnp.where((cluster == c)[None], level_ref[c, quantity(q)], own)
        rhs_ref[:, pl.ds(q * LANES, LANES)] = stationary(own)
    for d in range(3):
        w_ref[pl.ds(d * MODES, MODES), :] = streamed(stiff_ref[d].T)
    w_ref[pl.ds(3 * MODES, 4 * MODES), :] = streamed(lift_ref[...].reshape(4 * MODES, MODES))
    y = matmul(w_ref[...], rhs_ref[...])
    for q in range(QUANT):
        y_ref[q] = y[:, q * LANES : (q + 1) * LANES].reshape(7 * MT, SUB, LANES)

    def gather(q, carry):
        acc = state_ref[q].reshape(MT, SUB, LANES)
        for p in range(QUANT):
            for d in range(3):
                acc = acc + y_ref[p, pl.ds(d * MT, MT)] * row8(jac_ref, (p, q), d)
            for f in range(4):
                acc = acc - y_ref[p, pl.ds((3 + f) * MT, MT)] * row8(riem_ref, (0, p, q), f)
        part_ref[pl.ds(q * MT, MT)] = acc
        return carry

    lax.fori_loop(0, QUANT, gather, 0)
    row_ref[...] = jnp.zeros(row_ref.shape, i32)
    row_ref[:, : slot_ref.shape[1]] = spread(slot_ref[...])
    owned = cluster_ref.shape[1]
    for f in range(4):
        place = spread(partner_ref[f : f + 1, :])
        slot = jnp.maximum(place - owned, 0)
        idx = jnp.where(place < owned, place, pick(row_ref, slot))

        def local(q, carry, idx=idx, f=f):
            at = pl.ds(q * MT, MT)
            near = take(level_ref[0, at], idx)
            for c in range(1, LEVELS):
                near = jnp.where((cluster == c)[None], take(level_ref[c, at], idx), near)
            near_ref[f, at] = near
            return carry

        lax.fori_loop(0, QUANT, local, 0)
        wa_ref[f] = streamed(across_ref[f].reshape(4 * MODES, MODES))
    step = jnp.where(cluster == 0, base_step, jnp.where(cluster == 1, 2.0 * base_step, 4.0 * base_step))
    gain_ref[...] = spread(yield_ref[...].astype(f32)) * (1.0 - jnp.exp(-step / spread(relax_ref[...])))


def final_kernel(plan, *refs):
    gots = refs[: plan.count]
    (wish_ref, part_ref, near_ref, wa_ref, riem_ref, partner_ref, side_ref,
     cohesion_ref, gain_ref, out_ref, mixed_ref, rhs_ref, z_ref, chosen_ref) = refs[plan.count :]
    owned = partner_ref.shape[1]
    lane = lane_ids()
    bases = plan.bases()
    wishes = [
        wish_ref[...] if m == 0 else take(wish_ref[...], jnp.bitwise_xor(lane, m << plan.shift))
        for m in range(plan.masks)
    ]
    for r in range(plan.n_reg):
        mine = plan.members(r)
        block = {k: jnp.right_shift(lane, plan.width[k].bit_length() - 1) for k in mine}
        for v in range(VT):
            mixed = None
            for k in mine:
                chunk = plan.chunk(k)
                got = gots[k][v % chunk]
                if plan.full[k]:
                    for c in range(1, LEVELS):
                        got = jnp.where(wishes[plan.mask_id(v)] == c, gots[k][c * chunk + v % chunk], got)
                at = (plan.start[k] // plan.width[k]) ^ (v // chunk)
                mixed = got if mixed is None else jnp.where(block[k] == at, got, mixed)
            mixed_ref[r, v] = mixed
    for f in range(4):
        slot = spread(partner_ref[f : f + 1, :]) - owned
        spot = jnp.zeros((SUB, LANES), i32)
        where = jnp.zeros((SUB, LANES), i32) - 1
        for k in range(plan.count):
            rel = slot - bases[k]
            hit = jnp.logical_and(rel >= 0, rel < plan.width[k])
            spot = jnp.where(hit, rel + plan.start[k], spot)
            where = jnp.where(hit, plan.reg[k], where)
        spots = [jnp.bitwise_xor(spot, m << plan.shift) for m in range(plan.masks)]
        side = spread(side_ref[f : f + 1, :])
        for q in range(QUANT):
            parts = []
            for v in range(q * MT, (q + 1) * MT):
                near = near_ref[f, v]
                for r in range(plan.n_reg):
                    near = jnp.where(where == r, take(mixed_ref[r, v], spots[plan.mask_id(v)]), near)
                parts.append(near)
            rhs_ref[f, :, pl.ds(q * LANES, LANES)] = stationary(jnp.stack(parts))
        z = matmul(wa_ref[f], rhs_ref[f])
        for q in range(QUANT):
            column = z[:, q * LANES : (q + 1) * LANES].reshape(4, MT, SUB, LANES)
            chosen = column[0]
            for j in range(1, 4):
                chosen = jnp.where((side == j)[None], column[j], chosen)
            chosen_ref[f, q] = chosen

    def gather(q, carry):
        acc = part_ref[pl.ds(q * MT, MT)]
        for f in range(4):
            for p in range(QUANT):
                acc = acc - chosen_ref[f, p] * row8(riem_ref, (1, p, q), f)
        out_ref[q] = acc.reshape(MODES, LANES)
        return carry

    lax.fori_loop(0, QUANT, gather, 0)
    heads = [out_ref[q, 0:1, :] for q in range(6)]
    mean = (heads[0] + heads[1] + heads[2]) / 3.0
    dev = [heads[q] - mean if q < 3 else heads[q] for q in range(6)]
    second = 0.5 * (dev[0] * dev[0] + dev[1] * dev[1] + dev[2] * dev[2])
    second = second + dev[3] * dev[3] + dev[4] * dev[4] + dev[5] * dev[5]
    strength = jnp.sqrt(second)
    cohesion = cohesion_ref[...]
    excess = jnp.maximum(strength - cohesion, 0.0) / jnp.maximum(strength, cohesion)
    factor = spread(gain_ref[0:1, :] * excess)
    now = [out_ref[q].reshape(MT, SUB, LANES) for q in range(6)]
    pressure = (now[0] + now[1] + now[2]) / 3.0
    for q in range(6):
        fresh = now[q] - factor * (now[q] - pressure if q < 3 else now[q])
        out_ref[q] = fresh.reshape(MODES, LANES)


def call(kernel, plan, out_shape, scratch, *args, spaces=None, cost=None, name=None):
    vmem = pl.BlockSpec(memory_space=pltpu.VMEM)
    many = isinstance(out_shape, (list, tuple))

    def body(*refs):
        if plan is None:
            kernel(*refs)
        else:
            kernel(plan, *refs)

    return pl.pallas_call(
        body,
        out_shape=out_shape,
        in_specs=spaces or [vmem] * len(args),
        out_specs=[vmem] * len(out_shape) if many else vmem,
        scratch_shapes=scratch,
        compiler_params=pltpu.CompilerParams(vmem_limit_bytes=VMEM_LIMIT),
        cost_estimate=cost,
        name=name,
    )(*args)


def on_device(
    n_dom, n_grp, old_state, stiffness, jacobians, lift_own, lift_across, riemann,
    cluster_ids, send_slots, face_partner, partner_face, cohesion, relax_time, yield_flag,
):
    plan = Plan(n_dom, n_grp)
    owned = old_state.shape[2]
    slots = send_slots.shape[0]
    wide = round_up(slots, LANES)
    shape = jax.ShapeDtypeStruct
    jac = jnp.transpose(jacobians, (1, 2, 0, 3))
    riem = jnp.transpose(riemann, (0, 2, 3, 1, 4))
    cluster = cluster_ids.reshape(1, owned)
    slot_row = send_slots.reshape(1, slots)
    bulk = (old_state, stiffness, jac)

    early = (face_partner, cluster, *bulk)
    loaded = call(
        request_kernel, plan,
        [shape((SUB, LANES), i32)] * plan.count + [shape(a.shape, a.dtype) for a in bulk],
        [
            pltpu.VMEM(face_partner.shape, i32),
            pltpu.VMEM(cluster.shape, i32),
            pltpu.VMEM((SUB, wide), i32),
            pltpu.SemaphoreType.DMA((len(early),)),
        ],
        *early, spaces=[pl.BlockSpec(memory_space=pl.ANY)] * len(early), name="requests",
    )
    requests, (state_v, stiff_v, jac_v) = loaded[: plan.count], loaded[plan.count :]
    wanted = {}
    for k in plan.order:
        wanted[k] = lax.ppermute(requests[k], *plan.route[k])

    levels = call(
        predictor_kernel, None,
        shape((LEVELS, VP, SUB, LANES), f32),
        [
            pltpu.VMEM((3 * MODES, 3 * MODES), bf16),
            pltpu.VMEM((QUANT // GROUP + 1, 3 * MODES, GROUP * LANES), bf16),
            pltpu.VMEM((QUANT // GROUP + 1, GROUP, 3 * MT, SUB, LANES), f32),
            pltpu.VMEM((QUANT // GROUP + 1, GROUP, 3 * MT, SUB, LANES), f32),
        ],
        state_v, stiff_v, jac_v, name="predictor",
    )

    gots = [None] * plan.count
    for r in reversed(range(plan.n_reg)):
        mine = plan.members(r)
        asked = [wanted[k] for k in mine if not plan.full[k]]
        outgoing = call(
            lambda p, *refs, r=r: send_kernel(p, r, *refs), plan,
            [shape((plan.height(k), SUB, LANES), f32) for k in mine],
            [pltpu.VMEM((SUB, wide), i32)],
            levels, slot_row, *asked, name=f"sends_{r}",
        )
        for k, message in zip(mine, outgoing):
            gots[k] = lax.ppermute(message, *plan.route[k])

    partial, near, across, gain = call(
        own_kernel, plan,
        [
            shape((VT, SUB, LANES), f32),
            shape((4, VT, SUB, LANES), f32),
            shape((4, 4 * MODES, 3 * MODES), bf16),
            shape((SUB, LANES), f32),
        ],
        [
            pltpu.VMEM((SUB, wide), i32),
            pltpu.VMEM((7 * MODES, 3 * MODES), bf16),
            pltpu.VMEM((3 * MODES, QUANT * LANES), bf16),
            pltpu.VMEM((QUANT, 7 * MT, SUB, LANES), f32),
        ],
        levels, state_v, stiff_v, jac_v, lift_own, lift_across, riem, cluster, slot_row,
        face_partner, relax_time.reshape(1, owned), yield_flag.reshape(1, owned),
        cost=pl.CostEstimate(flops=10**8, bytes_accessed=4 * 10**6, transcendentals=0),
        name="own",
    )

    return call(
        final_kernel, plan,
        shape((QUANT, MODES, LANES), f32),
        [
            pltpu.VMEM((plan.n_reg, VT, SUB, LANES), f32),
            pltpu.VMEM((4, 3 * MODES, QUANT * LANES), bf16),
            pltpu.VMEM((4 * MODES, QUANT * LANES), f32),
            pltpu.VMEM((4, QUANT, MT, SUB, LANES), f32),
        ],
        *gots, requests[1], partial, near, across, riem, face_partner, partner_face,
        cohesion.reshape(1, owned), gain, name="final",
    )


def solution(mesh):
    n_dom, n_grp = mesh.shape["dom"], mesh.shape["grp"]
    both = ("dom", "grp")
    in_specs = (
        P(None, None, both), P(), P(None, None, None, both), P(), P(),
        P(None, None, None, None, both), P(both), P(both), P(None, both), P(None, both),
        P(both), P(both), P(both),
    )

    def body(*args):
        return on_device(n_dom, n_grp, *args)

    return jax.shard_map(
        body, mesh=mesh, in_specs=in_specs, out_specs=P(None, None, both), check_vma=False
    )
```
